512 devices in a mesh: pipe: 16 (over z_hi, y), expert: 32 (over z_lo, x, core).
Axes of the slice: x: 4, y: 4, z: 16 (z_hi: 4, z_lo: 4; z = z_hi * 4 + z_lo), core: 2. Of those that a mesh axis runs over, the one named last changes fastest.
Arguments:
- tokens: bfloat16 [16, 4096, 3584], P('pipe', 'expert'), may hold values from -6 to 6
- cotangent: bfloat16 [16, 4096, 3584], P('pipe', 'expert'), may hold values from -6 to 6
- routed: int32 [16, 4096, 2], P('pipe', 'expert'), may hold values from 0 to 1, as said below
- gate: float32 [16, 4096, 2], P('pipe', 'expert'), may hold values from 0.05 to 0.5
- up_weight: bfloat16 [3584, 4096], P(None, 'expert'), may hold values from -0.09375 to 0.09375
- down_weight: bfloat16 [4096, 3584], P('expert'), may hold values from -0.125 to 0.125
Outputs:
- up_grad: bfloat16 [16, 1792, 4096], P('pipe', None, 'expert')
- down_grad: bfloat16 [16, 4096, 1792], P('pipe', 'expert')
The draws below stay inside these ranges and needn't reach their ends.
Inputs may be any that keep to these rules, and one draw needn't show every extreme that they name: In each micro-batch and token block of 128 tokens, at most 16 tokens are routed to each expert in flight; in each micro-batch one expert, drawn from the seed, gets exactly 16 tokens from every block, and every expert gets exactly 16 from at least one block. A token may be routed to several experts in flight or to none.
All inputs are finite; a program needn't handle non-finite values.
Results may differ from the reference program's by a relative error of at most 0.02.
Values may be sent and summed in bfloat16 or wider, within the bound.
No kernel may reach another device: no remote copies, remote signals or barrier semaphores. Data moves between devices by JAX's collectives and lax.ppermute only.
A program may use at most 64 MiB of HBM per device.

```python
import math
import jax
import jax.numpy as jnp
from jax import lax

D = 3584
HID = 2048
EXPERTS = 2
TOK_DEV = 128
CAP = 16
TOKENS = 4096
N_PIPE = 16


def draw_routed(key, part):
    blocks = TOKENS // TOK_DEV
    key_hot, key_count, key_full, key_order = jax.random.split(key, 4)
    hottest = jax.random.randint(key_hot, (N_PIPE, 1, 1), 0, EXPERTS)
    counts = jax.random.randint(key_count, (N_PIPE, blocks, EXPERTS), 1, CAP + 1)
    full_block = jax.random.randint(key_full, (N_PIPE, 1, EXPERTS), 0, blocks)
    block_ids = jnp.arange(blocks, dtype=jnp.int32)[None, :, None]
    expert_ids = jnp.arange(EXPERTS, dtype=jnp.int32)[None, None, :]
    counts = jnp.where(block_ids == full_block, CAP, counts)
    counts = jnp.where(expert_ids == hottest, CAP, counts)
    scores = jax.random.randint(key_order, (N_PIPE, blocks, EXPERTS, TOK_DEV), 0, 2 ** 20)
    scores = scores * TOK_DEV + jnp.arange(TOK_DEV, dtype=jnp.int32)
    ranks = jnp.argsort(jnp.argsort(scores, axis=-1), axis=-1)
    chosen = jnp.where(ranks < counts[..., None], 1, 0).astype(jnp.int32)
    chosen = jnp.transpose(chosen, (0, 1, 3, 2))
    return chosen.reshape(N_PIPE, TOKENS, EXPERTS).astype(jnp.int32)


def steps_of(stream_key, shape, pieces, low, top_value):
    gain = 1.0
    for position, parts in pieces:
        heights = jax.random.uniform(jax.random.fold_in(jax.random.fold_in(stream_key, 6), position), (parts,), jnp.float32, low / len(pieces), top_value / len(pieces))
        gain = gain * jnp.repeat(jnp.exp(heights), shape[position] // parts).reshape((-1,) + (1,) * (len(shape) - 1 - position))
    return gain


def bell_draw(key, shape, scale, bound, pieces=(), kind=jnp.bfloat16):
    entries = jax.random.normal(key, shape, jnp.float32) * scale
    if len(pieces) > 0:
        entries = steps_of(key, shape, pieces, -0.22, 0.18) * entries
    return jnp.clip(entries, min=-bound, max=bound).astype(kind)


def setup_inputs(seed: int = 0) -> dict:
    arg_keys = jax.random.split(jax.random.key(seed), 7)
    return {
        "tokens": bell_draw(arg_keys[0], (N_PIPE, TOKENS, D), 1.0, 6.0, ((0, 16), (1, 32))),
        "cotangent": bell_draw(arg_keys[1], (N_PIPE, TOKENS, D), 1.0, 6.0, ((0, 16), (1, 32))),
        "routed": draw_routed(jax.random.fold_in(arg_keys[6], 71), 0),
        "gate": jnp.clip(jnp.exp(math.log(0.5) - 2.3025851 * jax.random.uniform(arg_keys[3], (N_PIPE, TOKENS, EXPERTS), jnp.float32) ** steps_of(arg_keys[3], (N_PIPE, TOKENS, EXPERTS), ((0, 16), (1, 32)), -0.2, 0.2)), 0.05, 0.5),
        "up_weight": bell_draw(arg_keys[4], (D, EXPERTS * HID), D ** -0.5, 0.09375, ((1, 32),)),
        "down_weight": bell_draw(arg_keys[5], (EXPERTS * HID, D), HID ** -0.5, 0.125, ((0, 32),)),
    }


def expert_grads(token_block, grad_block, routing, gating, up_weight, down_weight):
    slot_index = jnp.cumsum(routing, axis=1) - 1
    slot_ids = jnp.arange(CAP, dtype=jnp.int32)
    up_parts = []
    down_parts = []
    for expert in range(EXPERTS):
        chosen = (routing[:, None, :, expert] == 1) & (slot_index[:, None, :, expert] == slot_ids[None, :, None])
        picker = jnp.where(chosen, 1.0, 0.0).astype(jnp.float32)
        token_rows = jnp.einsum('bct,btd->bcd', picker, token_block.astype(jnp.float32)).astype(jnp.bfloat16).reshape(-1, D)
        plain_rows = jnp.einsum('bct,btd->bcd', picker, grad_block.astype(jnp.float32))
        slot_gate = jnp.einsum('bct,bt->bc', picker, gating[:, :, expert].astype(jnp.float32))
        grad_rows = (slot_gate[..., None] * plain_rows).astype(jnp.bfloat16).reshape(-1, D)
        w_up = up_weight[:, expert * HID:(expert + 1) * HID]
        w_down = down_weight[expert * HID:(expert + 1) * HID]
        upper = jnp.dot(token_rows, w_up, preferred_element_type=jnp.float32)
        hidden = jax.nn.silu(upper).astype(jnp.bfloat16)
        down_parts.append(jnp.dot(hidden.T, grad_rows, preferred_element_type=jnp.float32).astype(jnp.bfloat16))
        hidden_grad = jnp.dot(grad_rows, w_down.T, preferred_element_type=jnp.float32)
        sigma = jax.nn.sigmoid(upper)
        act_grad = (hidden_grad * sigma * (1.0 + upper * (1.0 - sigma))).astype(jnp.bfloat16)
        up_parts.append(jnp.dot(token_rows.T, act_grad, preferred_element_type=jnp.float32).astype(jnp.bfloat16))
    return jnp.concatenate(up_parts, axis=1), jnp.concatenate(down_parts, axis=0)


def reference(tokens, cotangent, routed, gate, up_weight, down_weight):
    sections = tokens.shape[0]
    blocks = TOKENS // TOK_DEV
    token_blocks = tokens.reshape(sections, blocks, TOK_DEV, D)
    grad_blocks = cotangent.reshape(sections, blocks, TOK_DEV, D)
    route_blocks = routed.reshape(sections, blocks, TOK_DEV, EXPERTS)
    gate_blocks = gate.reshape(sections, blocks, TOK_DEV, EXPERTS)

    def one_section(items):
        return expert_grads(items[0], items[1], items[2], items[3], up_weight, down_weight)

    section_up, section_down = lax.map(one_section, (token_blocks, grad_blocks, route_blocks, gate_blocks))
    half = sections // 2
    width = D // 2
    mirror_up = jnp.roll(section_up, half, axis=0)
    mirror_down = jnp.roll(section_down, half, axis=0)
    up_first = section_up[:half, :width].astype(jnp.float32) + mirror_up[:half, :width].astype(jnp.float32)
    up_second = section_up[half:, width:].astype(jnp.float32) + mirror_up[half:, width:].astype(jnp.float32)
    down_first = section_down[:half, :, :width].astype(jnp.float32) + mirror_down[:half, :, :width].astype(jnp.float32)
    down_second = section_down[half:, :, width:].astype(jnp.float32) + mirror_down[half:, :, width:].astype(jnp.float32)
    up_grad = jnp.concatenate([up_first, up_second], axis=0).astype(jnp.bfloat16)
    down_grad = jnp.concatenate([down_first, down_second], axis=0).astype(jnp.bfloat16)
    return (up_grad, down_grad)
```

```python
import jax
import jax.numpy as jnp
from jax import lax
from jax.experimental import pallas as pl
from jax.experimental.pallas import tpu as pltpu
from jax.sharding import PartitionSpec as P

CAP = 16
BF = jnp.bfloat16
FL = jnp.float32


def pick_rows(side_ref, tok_ref, cot_ref, routed_ref, gate_ref, own_t, other_t, own_g, other_g):
    side = side_ref[0]
    tokens = tok_ref.shape[0]
    routed = routed_ref[...]
    row_id = lax.broadcasted_iota(jnp.int32, (tokens, tokens), 0)
    col_id = lax.broadcasted_iota(jnp.int32, (tokens, tokens), 1)
    upper = jnp.where(row_id <= col_id, 1.0, 0.0).astype(BF)
    count = jnp.dot(routed.astype(FL).astype(BF), upper, preferred_element_type=FL)
    slot = count.astype(jnp.int32) - 1
    slot_ids = lax.broadcasted_iota(jnp.int32, (CAP, tokens), 0)

    def chosen(e):
        return (routed[e : e + 1] == 1) & (slot[e : e + 1] == slot_ids)

    first, second = chosen(0), chosen(1)
    gates = gate_ref[...]
    lean = jnp.full((CAP, tokens), side, jnp.int32) == 0
    one = jnp.where(first, 1.0, 0.0)
    two = jnp.where(second, 1.0, 0.0)
    mine = jnp.where(lean, one, two)
    rest = jnp.where(lean, two, one)
    gate_one = jnp.where(first, gates[0:1], 0.0)
    gate_two = jnp.where(second, gates[1:2], 0.0)
    gate_mine = jnp.sum(jnp.where(lean, gate_one, gate_two), axis=1, keepdims=True)
    gate_rest = jnp.sum(jnp.where(lean, gate_two, gate_one), axis=1, keepdims=True)
    picker = jnp.concatenate([mine, rest], axis=0).astype(BF)
    scale = jnp.concatenate([gate_mine, gate_rest], axis=0)
    rows = jnp.dot(picker, tok_ref[...], preferred_element_type=FL).astype(BF)
    own_t[...] = rows[:CAP]
    other_t[...] = rows[CAP:]
    grads = (jnp.dot(picker, cot_ref[...], preferred_element_type=FL) * scale).astype(BF)
    own_g[...] = grads[:CAP]
    other_g[...] = grads[CAP:]


def picked(side, tokens, cotangent, routed, gate):
    vmem = pl.BlockSpec(memory_space=pltpu.VMEM)
    out = jax.ShapeDtypeStruct((CAP, tokens.shape[1]), BF)
    return pl.pallas_call(
        pick_rows,
        in_specs=[pl.BlockSpec(memory_space=pltpu.SMEM), vmem, vmem, vmem, vmem],
        out_specs=(vmem,) * 4,
        out_shape=(out,) * 4,
    )(side[None], tokens, cotangent, routed, gate)


def shards(tokens, cotangent, routed, gate, up_weight, down_weight):
    members = lax.axis_size("expert")
    sections = lax.axis_size("pipe")
    width = tokens.shape[2]
    half = width // 2
    hid = up_weight.shape[1]

    def across(value, z_mask=0, x_mask=0, core_mask=0):
        flip = z_mask * 8 + x_mask * 2 + core_mask
        return lax.ppermute(value, "expert", [(s, s ^ flip) for s in range(members)])

    def mirrored(value):
        return lax.ppermute(value, "pipe", [(q, q ^ (sections // 2)) for q in range(sections)])

    member = lax.axis_index("expert")
    side = (member >= members // 2).astype(jnp.int32)
    upper = (lax.axis_index("pipe") >= sections // 2).astype(jnp.int32)
    own_start = upper * half
    sent_start = (1 - upper) * half

    def columns(value, start):
        return lax.dynamic_slice_in_dim(value, start, half, 1)

    own_t, other_t, own_g, other_g = picked(side, tokens[0], cotangent[0], routed[0].T, gate[0].T)

    far_t = across(other_t, z_mask=2)
    far_g = across(other_g, z_mask=2)
    near_t = jnp.concatenate([own_t, far_t], axis=0)
    near_g = jnp.concatenate([own_g, far_g], axis=0)
    pair_t = across(near_t, z_mask=1)
    pair_g = across(near_g, z_mask=1)

    other_up = across(up_weight, core_mask=1)
    other_down = across(down_weight, core_mask=1)
    wide_up = jnp.concatenate([up_weight, other_up], axis=1)
    wide_down = jnp.concatenate([down_weight, other_down], axis=0)

    def around(block):
        n = block.shape[0] // 2
        one = across(block, x_mask=1)
        three = across(block, x_mask=3)
        two_a = across(one[:n], x_mask=3)
        two_b = across(three[n:], x_mask=1)
        return one, three, two_a, two_b

    block_t = jnp.concatenate([near_t, pair_t], axis=0)
    block_g = jnp.concatenate([near_g, pair_g], axis=0)
    rows_t = jnp.concatenate([block_t, *around(block_t)], axis=0)
    rows_g = jnp.concatenate([block_g, *around(block_g)], axis=0)

    sent = jnp.concatenate([columns(near_t, sent_start), columns(near_g, sent_start)], axis=0)
    mirror_near = mirrored(sent)
    mirror_pair = across(mirror_near, z_mask=1)
    mirror_block = jnp.concatenate([mirror_near, mirror_pair], axis=0)
    m_one, m_three, m_two_a, m_two_b = around(mirror_block)
    n = CAP * 2
    m_t = jnp.concatenate(
        [part[k : k + n] for part in (mirror_block, m_one, m_three) for k in (0, 2 * n)] + [m_two_a[:n], m_two_b[:n]],
        axis=0,
    )
    m_g = jnp.concatenate(
        [part[k : k + n] for part in (mirror_block, m_one, m_three) for k in (n, 3 * n)] + [m_two_a[n:], m_two_b[n:]],
        axis=0,
    )

    up = jnp.dot(rows_t, wide_up, preferred_element_type=FL)
    sigma = jax.nn.sigmoid(up)
    hidden = (up * sigma).astype(BF)
    m_hidden = mirrored(hidden)
    hidden_grad = lax.dot_general(rows_g, wide_down, (((1,), (1,)), ((), ())), preferred_element_type=FL)
    act_grad = (hidden_grad * sigma * (1.0 + up * (1.0 - sigma))).astype(BF)
    m_act = mirrored(act_grad)

    all_hidden = jnp.concatenate([hidden, m_hidden], axis=0)
    all_act = jnp.concatenate([act_grad, m_act], axis=0)
    all_t = jnp.concatenate([columns(rows_t, own_start), m_t], axis=0)
    all_g = jnp.concatenate([columns(rows_g, own_start), m_g], axis=0)
    down = lax.dot_general(all_hidden, all_g, (((0,), (0,)), ((), ())), preferred_element_type=FL)
    down_in = across(down[hid:].astype(BF), core_mask=1)
    raise_ = lax.dot_general(all_t, all_act, (((0,), (0,)), ((), ())), preferred_element_type=FL)
    up_in = across(raise_[:, hid:].astype(BF), core_mask=1)
    down_out = (down[:hid] + down_in.astype(FL)).astype(BF)
    up_out = (raise_[:, :hid] + up_in.astype(FL)).astype(BF)
    return up_out[None], down_out[None]


def solution(mesh):
    in_specs = (
        P("pipe", "expert", None),
        P("pipe", "expert", None),
        P("pipe", "expert", None),
        P("pipe", "expert", None),
        P(None, "expert"),
        P("expert", None),
    )
    out_specs = (P("pipe", None, "expert"), P("pipe", "expert", None))
    return jax.shard_map(shards, mesh=mesh, in_specs=in_specs, out_specs=out_specs, check_vma=False)
```

```python
import jax
import jax.numpy as jnp
from jax import lax
from jax.experimental import pallas as pl
from jax.experimental.pallas import tpu as pltpu
from jax.sharding import PartitionSpec as P

CAP = 16
BF = jnp.bfloat16
FL = jnp.float32


def pick_rows(side_ref, tok_hbm, cot_hbm, routed_ref, gate_ref, own_ref, other_ref, tok_ref, cot_ref, sems):
    tok_copy = pltpu.make_async_copy(tok_hbm, tok_ref, sems.at[0])
    cot_copy = pltpu.make_async_copy(cot_hbm, cot_ref, sems.at[1])
    tok_copy.start()
    cot_copy.start()
    side = side_ref[0]
    tokens = tok_ref.shape[0]
    routed = routed_ref[...]
    row_id = lax.broadcasted_iota(jnp.int32, (tokens, tokens), 0)
    col_id = lax.broadcasted_iota(jnp.int32, (tokens, tokens), 1)
    upper = jnp.where(row_id <= col_id, 1.0, 0.0).astype(BF)
    count = jnp.dot(routed.astype(FL).astype(BF), upper, preferred_element_type=FL)
    slot = count.astype(jnp.int32) - 1
    slot_ids = lax.broadcasted_iota(jnp.int32, (CAP, tokens), 0)

    def chosen(e):
        return (routed[e : e + 1] == 1) & (slot[e : e + 1] == slot_ids)

    first, second = chosen(0), chosen(1)
    gates = gate_ref[...]
    lean = jnp.full((CAP, tokens), side, jnp.int32) == 0
    one = jnp.where(first, 1.0, 0.0)
    two = jnp.where(second, 1.0, 0.0)
    mine = jnp.where(lean, one, two)
    rest = jnp.where(lean, two, one)
    gate_one = jnp.where(first, gates[0:1], 0.0)
    gate_two = jnp.where(second, gates[1:2], 0.0)
    gate_mine = jnp.sum(jnp.where(lean, gate_one, gate_two), axis=1, keepdims=True)
    gate_rest = jnp.sum(jnp.where(lean, gate_two, gate_one), axis=1, keepdims=True)
    picker = jnp.concatenate([mine, rest], axis=0).astype(BF)
    scale = jnp.concatenate([gate_mine, gate_rest], axis=0)
    tok_copy.wait()
    rows = jnp.dot(picker, tok_ref[...], preferred_element_type=FL).astype(BF)
    own_ref[:CAP] = rows[:CAP]
    other_ref[:CAP] = rows[CAP:]
    cot_copy.wait()
    grads = (jnp.dot(picker, cot_ref[...], preferred_element_type=FL) * scale).astype(BF)
    own_ref[CAP:] = grads[:CAP]
    other_ref[CAP:] = grads[CAP:]


def picked(side, tokens, cotangent, routed, gate):
    vmem = pl.BlockSpec(memory_space=pltpu.VMEM)
    hbm = pl.BlockSpec(memory_space=pltpu.HBM)
    block = pltpu.VMEM(tokens.shape, BF)
    out = jax.ShapeDtypeStruct((2 * CAP, tokens.shape[1]), BF)
    return pl.pallas_call(
        pick_rows,
        in_specs=[pl.BlockSpec(memory_space=pltpu.SMEM), hbm, hbm, vmem, vmem],
        out_specs=(vmem,) * 2,
        out_shape=(out,) * 2,
        scratch_shapes=[block, block, pltpu.SemaphoreType.DMA((2,))],
        name="pick",
        compiler_params=pltpu.CompilerParams(vmem_limit_bytes=60 * 2**20),
    )(side[None], tokens, cotangent, routed, gate)


FREE = pl.CostEstimate(flops=0, transcendentals=0, bytes_accessed=0)
COPY = pl.CostEstimate(flops=0, transcendentals=0, bytes_accessed=10 * 2**20)
STEP = 512


def rows_to_units(rows, up_mine, up_other, down_mine, down_other, units):
    parts, tall, width = rows.shape
    starts = [(k, at) for k in range(parts) for at in range(0, tall, 2 * CAP)]
    up = grad = None
    for at in range(0, width, STEP):
        span = slice(at, at + STEP)
        wide_up = jnp.concatenate([up_mine[span], up_other[span]], axis=1)
        wide_down = jnp.concatenate([down_mine[:, span], down_other[:, span]], axis=0)
        rows_t = jnp.concatenate([rows[k, r : r + CAP, span] for k, r in starts], axis=0)
        rows_g = jnp.concatenate([rows[k, r + CAP : r + 2 * CAP, span] for k, r in starts], axis=0)
        more_up = jnp.dot(rows_t, wide_up, preferred_element_type=FL)
        more_grad = lax.dot_general(rows_g, wide_down, (((1,), (1,)), ((), ())), preferred_element_type=FL)
        up = more_up if up is None else up + more_up
        grad = more_grad if grad is None else grad + more_grad
    sigma = 1.0 / (1.0 + jnp.exp(-up))
    slots = up.shape[0]
    units[:slots] = (up * sigma).astype(BF)
    units[slots:] = (grad * sigma * (1.0 + up * (1.0 - sigma))).astype(BF)


def in_vmem(kernel, name, shape, *operands):
    vmem = pl.BlockSpec(memory_space=pltpu.VMEM)
    return pl.pallas_call(
        kernel,
        in_specs=[vmem] * len(operands),
        out_specs=vmem,
        out_shape=jax.ShapeDtypeStruct(shape, BF),
        name=name,
        cost_estimate=FREE,
        compiler_params=pltpu.CompilerParams(vmem_limit_bytes=20 * 2**20),
    )(*operands)


def repeat_block(first, second, out):
    n = first.shape[0]
    out[0, :n] = first[...]
    out[0, n:] = second[...]


def repeated(name, first, second):
    n, width = first.shape
    whole = pl.BlockSpec((n, width), lambda k: (0, 0))
    return pl.pallas_call(
        repeat_block,
        grid=(4,),
        in_specs=[whole, whole],
        out_specs=pl.BlockSpec((1, 2 * n, width), lambda k: (k, 0, 0)),
        out_shape=jax.ShapeDtypeStruct((4, 2 * n, width), BF),
        name=name,
        cost_estimate=COPY,
        compiler_params=pltpu.CompilerParams(vmem_limit_bytes=8 * 2**20),
    )(first, second)


def shards(tokens, cotangent, routed, gate, up_weight, down_weight):
    members = lax.axis_size("expert")
    sections = lax.axis_size("pipe")
    width = tokens.shape[2]
    half = width // 2
    hid = up_weight.shape[1]

    def across(name, value, z_mask=0, x_mask=0, core_mask=0):
        flip = z_mask * 8 + x_mask * 2 + core_mask
        with jax.named_scope(name):
            return lax.ppermute(value, "expert", [(s, s ^ flip) for s in range(members)])

    def mirrored(name, value):
        with jax.named_scope(name):
            return lax.ppermute(value, "pipe", [(q, q ^ (sections // 2)) for q in range(sections)])

    def after(value, other):
        return lax.optimization_barrier((value, other))

    member = lax.axis_index("expert")
    side = (member >= members // 2).astype(jnp.int32)
    upper = (lax.axis_index("pipe") >= sections // 2).astype(jnp.int32)
    own_start = upper * half
    sent_start = (1 - upper) * half

    def columns(value, start):
        return lax.dynamic_slice_in_dim(value, start, half, 1)

    own, other = picked(side, tokens[0], cotangent[0], routed[0].T, gate[0].T)

    circles = [[z + 2 * x for x in range(4)] for z in [8 * (k // 2) + k % 2 for k in range(members // 4)]]

    def ring(tag, first, second):
        with jax.named_scope(tag):
            copies = repeated(tag + "_copies", first, second)
            return lax.all_to_all(copies, "expert", 0, 0, axis_index_groups=circles, tiled=True)

    other_up = across("weight_up", up_weight, core_mask=1)
    other_down = across("weight_down", down_weight, core_mask=1)
    far = across("far", other, z_mask=2)
    beside = across("beside", own, z_mask=1)
    far, beside = after(far, beside)
    far_beside = across("far_beside", far, z_mask=1)

    sent = jnp.concatenate([columns(own, sent_start), columns(far, sent_start)], axis=0)
    far_beside, other_up, other_down = lax.optimization_barrier((far_beside, other_up, other_down))
    sent, far_beside = after(sent, far_beside)
    near_ring = ring("near_ring", own, far)
    pair_ring = ring("pair_ring", beside, far_beside)

    slots = 8 * CAP

    def through(name, rows, *weights):
        return in_vmem(rows_to_units, name, (2 * slots, 2 * hid), rows, *weights)

    near_units = through("near_units", near_ring, up_weight, other_up, down_weight, other_down)
    near_sent = mirrored("units_near", near_units)
    other_down, near_units = after(other_down, near_units)
    pair_units = through("pair_units", pair_ring, up_weight, other_up, down_weight, other_down)
    pair_sent = mirrored("units_pair", pair_units)

    mirror_near = mirrored("rows_mirror", sent)
    mirror_near, near_units = after(mirror_near, near_units)
    mirror_pair = across("pair_m", mirror_near, z_mask=1)
    mirror_ring = ring("mirror_ring", mirror_near, mirror_pair)
    near_ring, near_units = after(near_ring, near_units)
    pair_ring, near_sent, pair_units = lax.optimization_barrier((pair_ring, near_sent, pair_units))
    pair_sent, mirror_ring = after(pair_sent, mirror_ring)

    def gathered(kind):
        own_parts = [
            lax.dynamic_slice_in_dim(part.reshape(4, 2, 2, CAP, width)[:, :, kind], own_start, half, 3)
            for part in (near_ring, pair_ring)
        ]
        sent_rows = mirror_ring.reshape(4, 4, 2, CAP, half)[:, :, kind]
        parts = own_parts + [sent_rows[:, :2], sent_rows[:, 2:]]
        return jnp.concatenate([part.reshape(slots, half) for part in parts], axis=0)

    all_t = gathered(0)
    all_g = gathered(1)
    units = (near_units, pair_units, near_sent, pair_sent)
    all_hidden = jnp.concatenate([part[:slots] for part in units], axis=0)
    all_act = jnp.concatenate([part[slots:] for part in units], axis=0)
    down = lax.dot_general(all_hidden, all_g, (((0,), (0,)), ((), ())), preferred_element_type=FL)
    down_in = across("down_swap", down[hid:].astype(BF), core_mask=1)
    raise_ = lax.dot_general(all_t, all_act, (((0,), (0,)), ((), ())), preferred_element_type=FL)
    up_in = across("up_swap", raise_[:, hid:].astype(BF), core_mask=1)
    down_out = (down[:hid] + down_in.astype(FL)).astype(BF)
    up_out = (raise_[:, :hid] + up_in.astype(FL)).astype(BF)
    return up_out[None], down_out[None]


def solution(mesh):
    in_specs = (
        P("pipe", "expert", None),
        P("pipe", "expert", None),
        P("pipe", "expert", None),
        P("pipe", "expert", None),
        P(None, "expert"),
        P("expert", None),
    )
    out_specs = (P("pipe", None, "expert"), P("pipe", "expert", None))
    return jax.shard_map(shards, mesh=mesh, in_specs=in_specs, out_specs=out_specs, check_vma=False)
```

```python
import jax
import jax.numpy as jnp
from jax import lax
from jax.experimental import pallas as pl
from jax.experimental.pallas import tpu as pltpu
from jax.sharding import PartitionSpec as P

CAP = 16
BF = jnp.bfloat16
FL = jnp.float32


def pick_rows(side_ref, tok_ref, cot_ref, routed_ref, gate_ref, own_ref, other_ref):
    side = side_ref[0]
    tokens = tok_ref.shape[0]
    routed = routed_ref[...]
    row_id = lax.broadcasted_iota(jnp.int32, (tokens, tokens), 0)
    col_id = lax.broadcasted_iota(jnp.int32, (tokens, tokens), 1)
    upper = jnp.where(row_id <= col_id, 1.0, 0.0).astype(BF)
    count = jnp.dot(routed.astype(FL).astype(BF), upper, preferred_element_type=FL)
    slot = count.astype(jnp.int32) - 1
    slot_ids = lax.broadcasted_iota(jnp.int32, (CAP, tokens), 0)

    def chosen(e):
        return (routed[e : e + 1] == 1) & (slot[e : e + 1] == slot_ids)

    first, second = chosen(0), chosen(1)
    gates = gate_ref[...]
    lean = jnp.full((CAP, tokens), side, jnp.int32) == 0
    one = jnp.where(first, 1.0, 0.0)
    two = jnp.where(second, 1.0, 0.0)
    mine = jnp.where(lean, one, two)
    rest = jnp.where(lean, two, one)
    gate_one = jnp.where(first, gates[0:1], 0.0)
    gate_two = jnp.where(second, gates[1:2], 0.0)
    gate_mine = jnp.sum(jnp.where(lean, gate_one, gate_two), axis=1, keepdims=True)
    gate_rest = jnp.sum(jnp.where(lean, gate_two, gate_one), axis=1, keepdims=True)
    picker = jnp.concatenate([mine, rest], axis=0).astype(BF)
    scale = jnp.concatenate([gate_mine, gate_rest], axis=0)
    rows = jnp.dot(picker, tok_ref[...], preferred_element_type=FL).astype(BF)
    own_ref[:CAP] = rows[:CAP]
    other_ref[:CAP] = rows[CAP:]
    grads = (jnp.dot(picker, cot_ref[...], preferred_element_type=FL) * scale).astype(BF)
    own_ref[CAP:] = grads[:CAP]
    other_ref[CAP:] = grads[CAP:]


def picked(side, tokens, cotangent, routed, gate):
    vmem = pl.BlockSpec(memory_space=pltpu.VMEM)
    out = jax.ShapeDtypeStruct((2 * CAP, tokens.shape[1]), BF)
    return pl.pallas_call(
        pick_rows,
        in_specs=[pl.BlockSpec(memory_space=pltpu.SMEM), vmem, vmem, vmem, vmem],
        out_specs=(vmem,) * 2,
        out_shape=(out,) * 2,
        name="pick",
        compiler_params=pltpu.CompilerParams(vmem_limit_bytes=60 * 2**20),
    )(side[None], tokens, cotangent, routed, gate)


FREE = pl.CostEstimate(flops=0, transcendentals=0, bytes_accessed=0)
STEP = 512


def rows_to_units(rows, up_mine, up_other, down_mine, down_other, units):
    parts, tall, width = rows.shape
    n = tall // 2
    up = grad = None
    for at in range(0, width, STEP):
        span = slice(at, at + STEP)
        wide_up = jnp.concatenate([up_mine[span], up_other[span]], axis=1)
        wide_down = jnp.concatenate([down_mine[:, span], down_other[:, span]], axis=0)
        rows_t = jnp.concatenate([rows[k, :n, span] for k in range(parts)], axis=0)
        rows_g = jnp.concatenate([rows[k, n:, span] for k in range(parts)], axis=0)
        more_up = jnp.dot(rows_t, wide_up, preferred_element_type=FL)
        more_grad = lax.dot_general(rows_g, wide_down, (((1,), (1,)), ((), ())), preferred_element_type=FL)
        up = more_up if up is None else up + more_up
        grad = more_grad if grad is None else grad + more_grad
    sigma = 1.0 / (1.0 + jnp.exp(-up))
    slots = up.shape[0]
    units[:slots] = (up * sigma).astype(BF)
    units[slots:] = (grad * sigma * (1.0 + up * (1.0 - sigma))).astype(BF)


def in_vmem(kernel, name, shape, *operands):
    vmem = pl.BlockSpec(memory_space=pltpu.VMEM)
    return pl.pallas_call(
        kernel,
        in_specs=[vmem] * len(operands),
        out_specs=vmem,
        out_shape=jax.ShapeDtypeStruct(shape, BF),
        name=name,
        cost_estimate=FREE,
        compiler_params=pltpu.CompilerParams(vmem_limit_bytes=20 * 2**20),
    )(*operands)


def shards(tokens, cotangent, routed, gate, up_weight, down_weight):
    members = lax.axis_size("expert")
    sections = lax.axis_size("pipe")
    width = tokens.shape[2]
    half = width // 2
    hid = up_weight.shape[1]

    def across(name, value, z_mask=0, x_mask=0, core_mask=0):
        flip = z_mask * 8 + x_mask * 2 + core_mask
        with jax.named_scope(name):
            return lax.ppermute(value, "expert", [(s, s ^ flip) for s in range(members)])

    def mirrored(name, value):
        with jax.named_scope(name):
            return lax.ppermute(value, "pipe", [(q, q ^ (sections // 2)) for q in range(sections)])

    def after(value, other):
        return lax.optimization_barrier((value, other))

    member = lax.axis_index("expert")
    side = (member >= members // 2).astype(jnp.int32)
    upper = (lax.axis_index("pipe") >= sections // 2).astype(jnp.int32)
    own_start = upper * half
    sent_start = (1 - upper) * half

    def columns(value, start):
        return lax.dynamic_slice_in_dim(value, start, half, 1)

    own, other = picked(side, tokens[0], cotangent[0], routed[0].T, gate[0].T)

    circles = [[z + 2 * x for x in range(4)] for z in [8 * (k // 2) + k % 2 for k in range(members // 4)]]

    def ring(tag, block):
        with jax.named_scope(tag):
            copies = jnp.broadcast_to(block[None], (4, *block.shape))
            return lax.all_to_all(copies, "expert", 0, 0, axis_index_groups=circles, tiled=True)

    other_up = across("weight_up", up_weight, core_mask=1)
    other_down = across("weight_down", down_weight, core_mask=1)
    far = across("far", other, z_mask=2)
    beside = across("beside", own, z_mask=1)
    far_beside = across("far_beside", far, z_mask=1)
    far_beside, other_up, other_down = lax.optimization_barrier((far_beside, other_up, other_down))

    def joined(first, second):
        return jnp.concatenate([first[:CAP], second[:CAP], first[CAP:], second[CAP:]], axis=0)

    near = joined(own, far)
    sent, far_beside = after(columns(near, sent_start), far_beside)
    pair = joined(beside, far_beside)
    near_ring = ring("near_ring", near)
    pair_ring = ring("pair_ring", pair)
    n = 2 * CAP
    slots = 8 * CAP

    def through(name, rows, *weights):
        return in_vmem(rows_to_units, name, (2 * slots, 2 * hid), rows, *weights)

    near_units = through("near_units", near_ring, up_weight, other_up, down_weight, other_down)
    near_sent = mirrored("units_near", near_units)
    other_down, near_units = after(other_down, near_units)
    pair_units = through("pair_units", pair_ring, up_weight, other_up, down_weight, other_down)
    pair_sent = mirrored("units_pair", pair_units)

    mirror_near = mirrored("rows_mirror", sent)
    mirror_near, near_units = after(mirror_near, near_units)
    mirror_pair = across("pair_m", mirror_near, z_mask=1)
    mirror_ring = ring("mirror_ring", jnp.concatenate([mirror_near, mirror_pair], axis=0))
    near_ring, near_units = after(near_ring, near_units)
    pair_ring, near_sent, pair_units = lax.optimization_barrier((pair_ring, near_sent, pair_units))
    pair_sent, mirror_ring = after(pair_sent, mirror_ring)

    def gathered(at):
        own = [lax.dynamic_slice_in_dim(part[:, at : at + n], own_start, half, 2) for part in (near_ring, pair_ring)]
        sent = [mirror_ring[:, at + k : at + k + n] for k in (0, 2 * n)]
        return jnp.concatenate([part.reshape(slots, half) for part in own + sent], axis=0)

    all_t = gathered(0)
    all_g = gathered(n)
    units = (near_units, pair_units, near_sent, pair_sent)
    all_hidden = jnp.concatenate([part[:slots] for part in units], axis=0)
    all_act = jnp.concatenate([part[slots:] for part in units], axis=0)
    down = lax.dot_general(all_hidden, all_g, (((0,), (0,)), ((), ())), preferred_element_type=FL)
    down_in = across("down_swap", down[hid:].astype(BF), core_mask=1)
    raise_ = lax.dot_general(all_t, all_act, (((0,), (0,)), ((), ())), preferred_element_type=FL)
    up_in = across("up_swap", raise_[:, hid:].astype(BF), core_mask=1)
    down_out = (down[:hid] + down_in.astype(FL)).astype(BF)
    up_out = (raise_[:, :hid] + up_in.astype(FL)).astype(BF)
    return up_out[None], down_out[None]


def solution(mesh):
    in_specs = (
        P("pipe", "expert", None),
        P("pipe", "expert", None),
        P("pipe", "expert", None),
        P("pipe", "expert", None),
        P(None, "expert"),
        P("expert", None),
    )
    out_specs = (P("pipe", None, "expert"), P("pipe", "expert", None))
    return jax.shard_map(shards, mesh=mesh, in_specs=in_specs, out_specs=out_specs, check_vma=False)
```

```python
import jax
import jax.numpy as jnp
from jax import lax
from jax.experimental import pallas as pl
from jax.experimental.pallas import tpu as pltpu
from jax.sharding import PartitionSpec as P

CAP = 16
BF = jnp.bfloat16
FL = jnp.float32


def pick_rows(side_ref, tok_ref, cot_ref, routed_ref, gate_ref, own_ref, other_ref):
    side = side_ref[0]
    tokens = tok_ref.shape[0]
    routed = routed_ref[...]
    row_id = lax.broadcasted_iota(jnp.int32, (tokens, tokens), 0)
    col_id = lax.broadcasted_iota(jnp.int32, (tokens, tokens), 1)
    upper = jnp.where(row_id <= col_id, 1.0, 0.0).astype(BF)
    count = jnp.dot(routed.astype(FL).astype(BF), upper, preferred_element_type=FL)
    slot = count.astype(jnp.int32) - 1
    slot_ids = lax.broadcasted_iota(jnp.int32, (CAP, tokens), 0)

    def chosen(e):
        return (routed[e : e + 1] == 1) & (slot[e : e + 1] == slot_ids)

    first, second = chosen(0), chosen(1)
    gates = gate_ref[...]
    lean = jnp.full((CAP, tokens), side, jnp.int32) == 0
    one = jnp.where(first, 1.0, 0.0)
    two = jnp.where(second, 1.0, 0.0)
    mine = jnp.where(lean, one, two)
    rest = jnp.where(lean, two, one)
    gate_one = jnp.where(first, gates[0:1], 0.0)
    gate_two = jnp.where(second, gates[1:2], 0.0)
    gate_mine = jnp.sum(jnp.where(lean, gate_one, gate_two), axis=1, keepdims=True)
    gate_rest = jnp.sum(jnp.where(lean, gate_two, gate_one), axis=1, keepdims=True)
    picker = jnp.concatenate([mine, rest], axis=0).astype(BF)
    scale = jnp.concatenate([gate_mine, gate_rest], axis=0)
    rows = jnp.dot(picker, tok_ref[...], preferred_element_type=FL).astype(BF)
    own_ref[:CAP] = rows[:CAP]
    other_ref[:CAP] = rows[CAP:]
    grads = (jnp.dot(picker, cot_ref[...], preferred_element_type=FL) * scale).astype(BF)
    own_ref[CAP:] = grads[:CAP]
    other_ref[CAP:] = grads[CAP:]


def picked(side, tokens, cotangent, routed, gate):
    vmem = pl.BlockSpec(memory_space=pltpu.VMEM)
    out = jax.ShapeDtypeStruct((2 * CAP, tokens.shape[1]), BF)
    return pl.pallas_call(
        pick_rows,
        in_specs=[pl.BlockSpec(memory_space=pltpu.SMEM), vmem, vmem, vmem, vmem],
        out_specs=(vmem,) * 2,
        out_shape=(out,) * 2,
        name="pick",
        compiler_params=pltpu.CompilerParams(vmem_limit_bytes=60 * 2**20),
    )(side[None], tokens, cotangent, routed, gate)


FREE = pl.CostEstimate(flops=0, transcendentals=0, bytes_accessed=0)
STEP = 512


def rows_to_units(rows, up_mine, up_other, down_mine, down_other, units):
    parts, tall, width = rows.shape
    n = tall // 2
    up = grad = None
    for at in range(0, width, STEP):
        span = slice(at, at + STEP)
        wide_up = jnp.concatenate([up_mine[span], up_other[span]], axis=1)
        wide_down = jnp.concatenate([down_mine[:, span], down_other[:, span]], axis=0)
        rows_t = jnp.concatenate([rows[k, :n, span] for k in range(parts)], axis=0)
        rows_g = jnp.concatenate([rows[k, n:, span] for k in range(parts)], axis=0)
        more_up = jnp.dot(rows_t, wide_up, preferred_element_type=FL)
        more_grad = lax.dot_general(rows_g, wide_down, (((1,), (1,)), ((), ())), preferred_element_type=FL)
        up = more_up if up is None else up + more_up
        grad = more_grad if grad is None else grad + more_grad
    sigma = 1.0 / (1.0 + jnp.exp(-up))
    slots = up.shape[0]
    units[:slots] = (up * sigma).astype(BF)
    units[slots:] = (grad * sigma * (1.0 + up * (1.0 - sigma))).astype(BF)


def in_vmem(kernel, name, shape, *operands):
    vmem = pl.BlockSpec(memory_space=pltpu.VMEM)
    return pl.pallas_call(
        kernel,
        in_specs=[vmem] * len(operands),
        out_specs=vmem,
        out_shape=jax.ShapeDtypeStruct(shape, BF),
        name=name,
        cost_estimate=FREE,
        compiler_params=pltpu.CompilerParams(vmem_limit_bytes=20 * 2**20),
    )(*operands)


def shards(tokens, cotangent, routed, gate, up_weight, down_weight):
    members = lax.axis_size("expert")
    sections = lax.axis_size("pipe")
    width = tokens.shape[2]
    half = width // 2
    hid = up_weight.shape[1]

    def across(name, value, z_mask=0, x_mask=0, core_mask=0):
        flip = z_mask * 8 + x_mask * 2 + core_mask
        with jax.named_scope(name):
            return lax.ppermute(value, "expert", [(s, s ^ flip) for s in range(members)])

    def mirrored(name, value):
        with jax.named_scope(name):
            return lax.ppermute(value, "pipe", [(q, q ^ (sections // 2)) for q in range(sections)])

    def after(value, other):
        return lax.optimization_barrier((value, other))

    member = lax.axis_index("expert")
    side = (member >= members // 2).astype(jnp.int32)
    upper = (lax.axis_index("pipe") >= sections // 2).astype(jnp.int32)
    own_start = upper * half
    sent_start = (1 - upper) * half

    def columns(value, start):
        return lax.dynamic_slice_in_dim(value, start, half, 1)

    own, other = picked(side, tokens[0], cotangent[0], routed[0].T, gate[0].T)

    circles = [[z + 2 * x for x in range(4)] for z in [8 * (k // 2) + k % 2 for k in range(members // 4)]]

    def repeated(block):
        return jnp.broadcast_to(block[None], (4, *block.shape))

    def around(tag, copies):
        with jax.named_scope(tag):
            return lax.all_to_all(copies, "expert", 0, 0, axis_index_groups=circles, tiled=True)

    def ring(tag, block):
        return around(tag, repeated(block))

    other_up = across("weight_up", up_weight, core_mask=1)
    other_down = across("weight_down", down_weight, core_mask=1)
    far = across("far", other, z_mask=2)
    beside = across("beside", own, z_mask=1)
    far_beside = across("far_beside", far, z_mask=1)
    far_beside, other_up, other_down = lax.optimization_barrier((far_beside, other_up, other_down))

    def joined(first, second):
        return jnp.concatenate([first[:CAP], second[:CAP], first[CAP:], second[CAP:]], axis=0)

    near = joined(own, far)
    sent, far_beside = after(columns(near, sent_start), far_beside)
    pair = joined(beside, far_beside)
    near_ring = ring("near_ring", near)
    pair_ring = ring("pair_ring", pair)
    n = 2 * CAP
    slots = 8 * CAP

    def through(name, rows, *weights):
        return in_vmem(rows_to_units, name, (2 * slots, 2 * hid), rows, *weights)

    near_units = through("near_units", near_ring, up_weight, other_up, down_weight, other_down)
    near_sent = mirrored("units_near", near_units)
    other_down, near_units = after(other_down, near_units)
    pair_units = through("pair_units", pair_ring, up_weight, other_up, down_weight, other_down)

    mirror_near = mirrored("rows_mirror", sent)
    mirror_near, near_units = after(mirror_near, near_units)
    mirror_pair = across("pair_m", mirror_near, z_mask=1)
    mirror_pair, pair_units = after(mirror_pair, pair_units)
    mirror_copies, pair_units, pair_ring = lax.optimization_barrier(
        (repeated(jnp.concatenate([mirror_near, mirror_pair], axis=0)), pair_units, pair_ring)
    )
    mirror_ring = around("mirror_ring", mirror_copies)
    pair_cols, pair_units = after(lax.dynamic_slice_in_dim(pair_ring[:, n:], own_start, half, 2), pair_units)
    pair_sent = mirrored("units_pair", pair_units)
    near_ring, near_units = after(near_ring, near_units)
    near_sent, pair_sent, mirror_ring = lax.optimization_barrier((near_sent, pair_sent, mirror_ring))

    def own_columns(part, at):
        return lax.dynamic_slice_in_dim(part[:, at : at + n], own_start, half, 2)

    def gathered(at):
        own = [own_columns(near_ring, at), own_columns(pair_ring, at) if at == 0 else pair_cols]
        sent = [mirror_ring[:, at + k : at + k + n] for k in (0, 2 * n)]
        return jnp.concatenate([part.reshape(slots, half) for part in own + sent], axis=0)

    all_t = gathered(0)
    all_g = gathered(n)
    units = (near_units, pair_units, near_sent, pair_sent)
    all_hidden = jnp.concatenate([part[:slots] for part in units], axis=0)
    all_act = jnp.concatenate([part[slots:] for part in units], axis=0)
    down = lax.dot_general(all_hidden, all_g, (((0,), (0,)), ((), ())), preferred_element_type=FL)
    down_in = across("down_swap", down[hid:].astype(BF), core_mask=1)
    raise_ = lax.dot_general(all_t, all_act, (((0,), (0,)), ((), ())), preferred_element_type=FL)
    up_in = across("up_swap", raise_[:, hid:].astype(BF), core_mask=1)
    down_out = (down[:hid] + down_in.astype(FL)).astype(BF)
    up_out = (raise_[:, :hid] + up_in.astype(FL)).astype(BF)
    return up_out[None], down_out[None]


def solution(mesh):
    in_specs = (
        P("pipe", "expert", None),
        P("pipe", "expert", None),
        P("pipe", "expert", None),
        P("pipe", "expert", None),
        P(None, "expert"),
        P("expert", None),
    )
    out_specs = (P("pipe", None, "expert"), P("pipe", "expert", None))
    return jax.shard_map(shards, mesh=mesh, in_specs=in_specs, out_specs=out_specs, check_vma=False)
```

```python
import jax
import jax.numpy as jnp
from jax import lax
from jax.experimental import pallas as pl
from jax.experimental.pallas import tpu as pltpu
from jax.sharding import PartitionSpec as P

CAP = 16
BF = jnp.bfloat16
FL = jnp.float32


def pick_rows(side_ref, tok_ref, cot_ref, routed_ref, gate_ref, own_ref, other_ref):
    side = side_ref[0]
    tokens = tok_ref.shape[0]
    routed = routed_ref[...]
    row_id = lax.broadcasted_iota(jnp.int32, (tokens, tokens), 0)
    col_id = lax.broadcasted_iota(jnp.int32, (tokens, tokens), 1)
    upper = jnp.where(row_id <= col_id, 1.0, 0.0).astype(BF)
    count = jnp.dot(routed.astype(FL).astype(BF), upper, preferred_element_type=FL)
    slot = count.astype(jnp.int32) - 1
    slot_ids = lax.broadcasted_iota(jnp.int32, (CAP, tokens), 0)

    def chosen(e):
        return (routed[e : e + 1] == 1) & (slot[e : e + 1] == slot_ids)

    first, second = chosen(0), chosen(1)
    gates = gate_ref[...]
    lean = jnp.full((CAP, tokens), side, jnp.int32) == 0
    one = jnp.where(first, 1.0, 0.0)
    two = jnp.where(second, 1.0, 0.0)
    mine = jnp.where(lean, one, two)
    rest = jnp.where(lean, two, one)
    gate_one = jnp.where(first, gates[0:1], 0.0)
    gate_two = jnp.where(second, gates[1:2], 0.0)
    gate_mine = jnp.sum(jnp.where(lean, gate_one, gate_two), axis=1, keepdims=True)
    gate_rest = jnp.sum(jnp.where(lean, gate_two, gate_one), axis=1, keepdims=True)
    picker = jnp.concatenate([mine, rest], axis=0).astype(BF)
    scale = jnp.concatenate([gate_mine, gate_rest], axis=0)
    rows = jnp.dot(picker, tok_ref[...], preferred_element_type=FL).astype(BF)
    own_ref[:CAP] = rows[:CAP]
    other_ref[:CAP] = rows[CAP:]
    grads = (jnp.dot(picker, cot_ref[...], preferred_element_type=FL) * scale).astype(BF)
    own_ref[CAP:] = grads[:CAP]
    other_ref[CAP:] = grads[CAP:]


def picked(side, tokens, cotangent, routed, gate):
    vmem = pl.BlockSpec(memory_space=pltpu.VMEM)
    out = jax.ShapeDtypeStruct((2 * CAP, tokens.shape[1]), BF)
    return pl.pallas_call(
        pick_rows,
        in_specs=[pl.BlockSpec(memory_space=pltpu.SMEM), vmem, vmem, vmem, vmem],
        out_specs=(vmem,) * 2,
        out_shape=(out,) * 2,
        name="pick",
        compiler_params=pltpu.CompilerParams(vmem_limit_bytes=60 * 2**20),
    )(side[None], tokens, cotangent, routed, gate)


FREE = pl.CostEstimate(flops=0, transcendentals=0, bytes_accessed=0)
STEP = 512


def rows_to_units(rows, up_mine, up_other, down_mine, down_other, units):
    parts, tall, width = rows.shape
    n = tall // 2
    up = grad = None
    for at in range(0, width, STEP):
        span = slice(at, at + STEP)
        wide_up = jnp.concatenate([up_mine[span], up_other[span]], axis=1)
        wide_down = jnp.concatenate([down_mine[:, span], down_other[:, span]], axis=0)
        rows_t = jnp.concatenate([rows[k, :n, span] for k in range(parts)], axis=0)
        rows_g = jnp.concatenate([rows[k, n:, span] for k in range(parts)], axis=0)
        more_up = jnp.dot(rows_t, wide_up, preferred_element_type=FL)
        more_grad = lax.dot_general(rows_g, wide_down, (((1,), (1,)), ((), ())), preferred_element_type=FL)
        up = more_up if up is None else up + more_up
        grad = more_grad if grad is None else grad + more_grad
    sigma = 1.0 / (1.0 + jnp.exp(-up))
    slots = up.shape[0]
    units[:slots] = (up * sigma).astype(BF)
    units[slots:] = (grad * sigma * (1.0 + up * (1.0 - sigma))).astype(BF)


def in_vmem(kernel, name, shape, *operands):
    vmem = pl.BlockSpec(memory_space=pltpu.VMEM)
    return pl.pallas_call(
        kernel,
        in_specs=[vmem] * len(operands),
        out_specs=vmem,
        out_shape=jax.ShapeDtypeStruct(shape, BF),
        name=name,
        cost_estimate=FREE,
        compiler_params=pltpu.CompilerParams(vmem_limit_bytes=20 * 2**20),
    )(*operands)


def shards(tokens, cotangent, routed, gate, up_weight, down_weight):
    members = lax.axis_size("expert")
    sections = lax.axis_size("pipe")
    width = tokens.shape[2]
    half = width // 2
    hid = up_weight.shape[1]

    def across(name, value, z_mask=0, x_mask=0, core_mask=0):
        flip = z_mask * 8 + x_mask * 2 + core_mask
        with jax.named_scope(name):
            return lax.ppermute(value, "expert", [(s, s ^ flip) for s in range(members)])

    def mirrored(name, value):
        with jax.named_scope(name):
            return lax.ppermute(value, "pipe", [(q, q ^ (sections // 2)) for q in range(sections)])

    def after(value, other):
        return lax.optimization_barrier((value, other))

    member = lax.axis_index("expert")
    side = (member >= members // 2).astype(jnp.int32)
    upper = (lax.axis_index("pipe") >= sections // 2).astype(jnp.int32)
    own_start = upper * half
    sent_start = (1 - upper) * half

    def columns(value, start):
        return lax.dynamic_slice_in_dim(value, start, half, 1)

    own, other = picked(side, tokens[0], cotangent[0], routed[0].T, gate[0].T)

    circles = [[z + 2 * x for x in range(4)] for z in [8 * (k // 2) + k % 2 for k in range(members // 4)]]

    def repeated(block):
        return jnp.broadcast_to(block[None], (4, *block.shape))

    def around(tag, copies):
        with jax.named_scope(tag):
            return lax.all_to_all(copies, "expert", 0, 0, axis_index_groups=circles, tiled=True)

    def ring(tag, block):
        return around(tag, repeated(block))

    other_up = across("weight_up", up_weight, core_mask=1)
    other_down = across("weight_down", down_weight, core_mask=1)
    far = across("far", other, z_mask=2)
    beside = across("beside", own, z_mask=1)
    far_beside = across("far_beside", far, z_mask=1)
    far_beside, other_up, other_down = lax.optimization_barrier((far_beside, other_up, other_down))

    def joined(first, second):
        return jnp.concatenate([first[:CAP], second[:CAP], first[CAP:], second[CAP:]], axis=0)

    near = joined(own, far)
    sent, far_beside = after(columns(near, sent_start), far_beside)
    pair = joined(beside, far_beside)
    near_ring = ring("near_ring", near)
    pair_ring = ring("pair_ring", pair)
    n = 2 * CAP
    slots = 8 * CAP

    def through(name, rows, *weights):
        return in_vmem(rows_to_units, name, (2 * slots, 2 * hid), rows, *weights)

    near_units = through("near_units", near_ring, up_weight, other_up, down_weight, other_down)
    near_sent = mirrored("units_near", near_units)
    other_down, near_units = after(other_down, near_units)
    pair_units = through("pair_units", pair_ring, up_weight, other_up, down_weight, other_down)

    mirror_near = mirrored("rows_mirror", sent)
    mirror_near, near_units = after(mirror_near, near_units)
    mirror_pair = across("pair_m", mirror_near, z_mask=1)
    mirror_pair, pair_units = after(mirror_pair, pair_units)
    mirror_copies, pair_units, pair_ring = lax.optimization_barrier(
        (repeated(jnp.concatenate([mirror_near, mirror_pair], axis=0)), pair_units, pair_ring)
    )
    mirror_ring = around("mirror_ring", mirror_copies)
    pair_cols, pair_units = after(lax.dynamic_slice(pair_ring, (0, n, own_start), (1, n, half)), pair_units)
    pair_sent = mirrored("units_pair", pair_units)
    near_ring, near_units = after(near_ring, near_units)
    near_sent, pair_sent, mirror_ring = lax.optimization_barrier((near_sent, pair_sent, mirror_ring))

    def own_columns(part, at):
        return lax.dynamic_slice(part, (0, at, own_start), (4, n, half))

    def gathered(at):
        own = [own_columns(near_ring, at)]
        own += [own_columns(pair_ring, at)] if at == 0 else [pair_cols, lax.dynamic_slice(pair_ring, (1, n, own_start), (3, n, half))]
        sent = [mirror_ring[:, at + k : at + k + n] for k in (0, 2 * n)]
        return jnp.concatenate([part.reshape(-1, half) for part in own + sent], axis=0)

    all_t = gathered(0)
    all_g = gathered(n)
    units = (near_units, pair_units, near_sent, pair_sent)
    all_hidden = jnp.concatenate([part[:slots] for part in units], axis=0)
    all_act = jnp.concatenate([part[slots:] for part in units], axis=0)
    down = lax.dot_general(all_hidden, all_g, (((0,), (0,)), ((), ())), preferred_element_type=FL)
    down_in = across("down_swap", down[hid:].astype(BF), core_mask=1)
    raise_ = lax.dot_general(all_t, all_act, (((0,), (0,)), ((), ())), preferred_element_type=FL)
    up_in = across("up_swap", raise_[:, hid:].astype(BF), core_mask=1)
    down_out = (down[:hid] + down_in.astype(FL)).astype(BF)
    up_out = (raise_[:, :hid] + up_in.astype(FL)).astype(BF)
    return up_out[None], down_out[None]


def solution(mesh):
    in_specs = (
        P("pipe", "expert", None),
        P("pipe", "expert", None),
        P("pipe", "expert", None),
        P("pipe", "expert", None),
        P(None, "expert"),
        P("expert", None),
    )
    out_specs = (P("pipe", None, "expert"), P("pipe", "expert", None))
    return jax.shard_map(shards, mesh=mesh, in_specs=in_specs, out_specs=out_specs, check_vma=False)
```

```python
import jax
import jax.numpy as jnp
from jax import lax
from jax.experimental import pallas as pl
from jax.experimental.pallas import tpu as pltpu
from jax.sharding import PartitionSpec as P

CAP = 16
BF = jnp.bfloat16
FL = jnp.float32


def pick_rows(side_ref, tok_ref, cot_ref, routed_ref, gate_ref, own_ref, other_ref):
    side = side_ref[0]
    tokens = tok_ref.shape[0]
    routed = routed_ref[...]
    row_id = lax.broadcasted_iota(jnp.int32, (tokens, tokens), 0)
    col_id = lax.broadcasted_iota(jnp.int32, (tokens, tokens), 1)
    upper = jnp.where(row_id <= col_id, 1.0, 0.0).astype(BF)
    count = jnp.dot(routed.astype(FL).astype(BF), upper, preferred_element_type=FL)
    slot = count.astype(jnp.int32) - 1
    slot_ids = lax.broadcasted_iota(jnp.int32, (CAP, tokens), 0)

    def chosen(e):
        return (routed[e : e + 1] == 1) & (slot[e : e + 1] == slot_ids)

    first, second = chosen(0), chosen(1)
    gates = gate_ref[...]
    lean = jnp.full((CAP, tokens), side, jnp.int32) == 0
    one = jnp.where(first, 1.0, 0.0)
    two = jnp.where(second, 1.0, 0.0)
    mine = jnp.where(lean, one, two)
    rest = jnp.where(lean, two, one)
    gate_one = jnp.where(first, gates[0:1], 0.0)
    gate_two = jnp.where(second, gates[1:2], 0.0)
    gate_mine = jnp.sum(jnp.where(lean, gate_one, gate_two), axis=1, keepdims=True)
    gate_rest = jnp.sum(jnp.where(lean, gate_two, gate_one), axis=1, keepdims=True)
    picker = jnp.concatenate([mine, rest], axis=0).astype(BF)
    scale = jnp.concatenate([gate_mine, gate_rest], axis=0)
    rows = jnp.dot(picker, tok_ref[...], preferred_element_type=FL).astype(BF)
    own_ref[:CAP] = rows[:CAP]
    other_ref[:CAP] = rows[CAP:]
    grads = (jnp.dot(picker, cot_ref[...], preferred_element_type=FL) * scale).astype(BF)
    own_ref[CAP:] = grads[:CAP]
    other_ref[CAP:] = grads[CAP:]


def picked(side, tokens, cotangent, routed, gate):
    vmem = pl.BlockSpec(memory_space=pltpu.VMEM)
    out = jax.ShapeDtypeStruct((2 * CAP, tokens.shape[1]), BF)
    return pl.pallas_call(
        pick_rows,
        in_specs=[pl.BlockSpec(memory_space=pltpu.SMEM), vmem, vmem, vmem, vmem],
        out_specs=(vmem,) * 2,
        out_shape=(out,) * 2,
        name="pick",
        compiler_params=pltpu.CompilerParams(vmem_limit_bytes=60 * 2**20),
    )(side[None], tokens, cotangent, routed, gate)


FREE = pl.CostEstimate(flops=0, transcendentals=0, bytes_accessed=0)
STEP = 512


def rows_to_units(rows, up_mine, up_other, down_mine, down_other, units):
    parts, tall, width = rows.shape
    n = tall // 2
    up = grad = None
    for at in range(0, width, STEP):
        span = slice(at, at + STEP)
        wide_up = jnp.concatenate([up_mine[span], up_other[span]], axis=1)
        wide_down = jnp.concatenate([down_mine[:, span], down_other[:, span]], axis=0)
        rows_t = jnp.concatenate([rows[k, :n, span] for k in range(parts)], axis=0)
        rows_g = jnp.concatenate([rows[k, n:, span] for k in range(parts)], axis=0)
        more_up = jnp.dot(rows_t, wide_up, preferred_element_type=FL)
        more_grad = lax.dot_general(rows_g, wide_down, (((1,), (1,)), ((), ())), preferred_element_type=FL)
        up = more_up if up is None else up + more_up
        grad = more_grad if grad is None else grad + more_grad
    sigma = 1.0 / (1.0 + jnp.exp(-up))
    slots = up.shape[0]
    units[:slots] = (up * sigma).astype(BF)
    units[slots:] = (grad * sigma * (1.0 + up * (1.0 - sigma))).astype(BF)


def in_vmem(kernel, name, shape, *operands):
    vmem = pl.BlockSpec(memory_space=pltpu.VMEM)
    return pl.pallas_call(
        kernel,
        in_specs=[vmem] * len(operands),
        out_specs=vmem,
        out_shape=jax.ShapeDtypeStruct(shape, BF),
        name=name,
        cost_estimate=FREE,
        compiler_params=pltpu.CompilerParams(vmem_limit_bytes=20 * 2**20),
    )(*operands)


def shards(tokens, cotangent, routed, gate, up_weight, down_weight):
    members = lax.axis_size("expert")
    sections = lax.axis_size("pipe")
    width = tokens.shape[2]
    half = width // 2
    hid = up_weight.shape[1]

    def across(name, value, z_mask=0, x_mask=0, core_mask=0):
        flip = z_mask * 8 + x_mask * 2 + core_mask
        with jax.named_scope(name):
            return lax.ppermute(value, "expert", [(s, s ^ flip) for s in range(members)])

    def mirrored(name, value):
        with jax.named_scope(name):
            return lax.ppermute(value, "pipe", [(q, q ^ (sections // 2)) for q in range(sections)])

    def after(value, other):
        return lax.optimization_barrier((value, other))

    member = lax.axis_index("expert")
    side = (member >= members // 2).astype(jnp.int32)
    upper = (lax.axis_index("pipe") >= sections // 2).astype(jnp.int32)
    own_start = upper * half
    sent_start = (1 - upper) * half

    def columns(value, start):
        return lax.dynamic_slice_in_dim(value, start, half, 1)

    own, other = picked(side, tokens[0], cotangent[0], routed[0].T, gate[0].T)

    circles = [[z + 2 * x for x in range(4)] for z in [8 * (k // 2) + k % 2 for k in range(members // 4)]]

    def repeated(block):
        return jnp.broadcast_to(block[None], (4, *block.shape))

    def around(tag, copies):
        with jax.named_scope(tag):
            return lax.all_to_all(copies, "expert", 0, 0, axis_index_groups=circles, tiled=True)

    def ring(tag, block):
        return around(tag, repeated(block))

    other_up = across("weight_up", up_weight, core_mask=1)
    other_down = across("weight_down", down_weight, core_mask=1)
    far = across("far", other, z_mask=2)
    beside = across("beside", own, z_mask=1)
    far_beside = across("far_beside", far, z_mask=1)
    far_beside, other_up, other_down = lax.optimization_barrier((far_beside, other_up, other_down))

    def joined(first, second):
        return jnp.concatenate([first[:CAP], second[:CAP], first[CAP:], second[CAP:]], axis=0)

    near = joined(own, far)
    sent, far_beside = after(columns(near, sent_start), far_beside)
    pair = joined(beside, far_beside)
    near_ring = ring("near_ring", near)
    pair_ring = ring("pair_ring", pair)
    n = 2 * CAP
    slots = 8 * CAP

    def through(name, rows, *weights):
        return in_vmem(rows_to_units, name, (2 * slots, 2 * hid), rows, *weights)

    near_units = through("near_units", near_ring, up_weight, other_up, down_weight, other_down)
    near_sent = mirrored("units_near", near_units)
    other_down, near_units = after(other_down, near_units)
    pair_units = through("pair_units", pair_ring, up_weight, other_up, down_weight, other_down)

    mirror_near = mirrored("rows_mirror", sent)
    mirror_near, near_units = after(mirror_near, near_units)
    mirror_pair = across("pair_m", mirror_near, z_mask=1)
    mirror_pair, pair_units = after(mirror_pair, pair_units)
    mirror_copies, pair_units, pair_ring = lax.optimization_barrier(
        (repeated(jnp.concatenate([mirror_near, mirror_pair], axis=0)), pair_units, pair_ring)
    )
    mirror_ring = around("mirror_ring", mirror_copies)
    pair_cols, pair_units = after(lax.dynamic_slice(pair_ring, (0, n, own_start), (1, n, half)), pair_units)
    pair_sent = mirrored("units_pair", pair_units)
    near_ring, near_units = after(near_ring, near_units)
    near_sent, pair_sent, mirror_ring = lax.optimization_barrier((near_sent, pair_sent, mirror_ring))

    def own_columns(part, at):
        return lax.dynamic_slice_in_dim(part[:, at : at + n], own_start, half, 2)

    def gathered(at):
        own = [own_columns(near_ring, at)]
        own += [own_columns(pair_ring, at)] if at == 0 else [pair_cols, lax.dynamic_slice(pair_ring, (1, n, own_start), (3, n, half))]
        sent = [mirror_ring[:, at + k : at + k + n] for k in (0, 2 * n)]
        return jnp.concatenate([part.reshape(-1, half) for part in own + sent], axis=0)

    all_t = gathered(0)
    all_g = gathered(n)
    units = (near_units, pair_units, near_sent, pair_sent)
    all_hidden = jnp.concatenate([part[:slots] for part in units], axis=0)
    all_act = jnp.concatenate([part[slots:] for part in units], axis=0)
    down = lax.dot_general(all_hidden, all_g, (((0,), (0,)), ((), ())), preferred_element_type=FL)
    down_in = across("down_swap", down[hid:].astype(BF), core_mask=1)
    raise_ = lax.dot_general(all_t, all_act, (((0,), (0,)), ((), ())), preferred_element_type=FL)
    up_in = across("up_swap", raise_[:, hid:].astype(BF), core_mask=1)
    down_out = (down[:hid] + down_in.astype(FL)).astype(BF)
    up_out = (raise_[:, :hid] + up_in.astype(FL)).astype(BF)
    return up_out[None], down_out[None]


def solution(mesh):
    in_specs = (
        P("pipe", "expert", None),
        P("pipe", "expert", None),
        P("pipe", "expert", None),
        P("pipe", "expert", None),
        P(None, "expert"),
        P("expert", None),
    )
    out_specs = (P("pipe", None, "expert"), P("pipe", "expert", None))
    return jax.shard_map(shards, mesh=mesh, in_specs=in_specs, out_specs=out_specs, check_vma=False)
```

```python
import jax
import jax.numpy as jnp
from jax import lax
from jax.experimental import pallas as pl
from jax.experimental.pallas import tpu as pltpu
from jax.sharding import PartitionSpec as P

CAP = 16
BF = jnp.bfloat16
FL = jnp.float32


def pick_rows(side_ref, tok_ref, cot_ref, routed_ref, gate_ref, own_ref, other_ref):
    side = side_ref[0]
    tokens = tok_ref.shape[0]
    routed = routed_ref[...]
    row_id = lax.broadcasted_iota(jnp.int32, (tokens, tokens), 0)
    col_id = lax.broadcasted_iota(jnp.int32, (tokens, tokens), 1)
    upper = jnp.where(row_id <= col_id, 1.0, 0.0).astype(BF)
    count = jnp.dot(routed.astype(FL).astype(BF), upper, preferred_element_type=FL)
    slot = count.astype(jnp.int32) - 1
    slot_ids = lax.broadcasted_iota(jnp.int32, (CAP, tokens), 0)

    def chosen(e):
        return (routed[e : e + 1] == 1) & (slot[e : e + 1] == slot_ids)

    first, second = chosen(0), chosen(1)
    gates = gate_ref[...]
    lean = jnp.full((CAP, tokens), side, jnp.int32) == 0
    one = jnp.where(first, 1.0, 0.0)
    two = jnp.where(second, 1.0, 0.0)
    mine = jnp.where(lean, one, two)
    rest = jnp.where(lean, two, one)
    gate_one = jnp.where(first, gates[0:1], 0.0)
    gate_two = jnp.where(second, gates[1:2], 0.0)
    gate_mine = jnp.sum(jnp.where(lean, gate_one, gate_two), axis=1, keepdims=True)
    gate_rest = jnp.sum(jnp.where(lean, gate_two, gate_one), axis=1, keepdims=True)
    picker = jnp.concatenate([mine, rest], axis=0).astype(BF)
    scale = jnp.concatenate([gate_mine, gate_rest], axis=0)
    rows = jnp.dot(picker, tok_ref[...], preferred_element_type=FL).astype(BF)
    own_ref[:CAP] = rows[:CAP]
    other_ref[:CAP] = rows[CAP:]
    grads = (jnp.dot(picker, cot_ref[...], preferred_element_type=FL) * scale).astype(BF)
    own_ref[CAP:] = grads[:CAP]
    other_ref[CAP:] = grads[CAP:]


def picked(side, tokens, cotangent, routed, gate):
    vmem = pl.BlockSpec(memory_space=pltpu.VMEM)
    out = jax.ShapeDtypeStruct((2 * CAP, tokens.shape[1]), BF)
    return pl.pallas_call(
        pick_rows,
        in_specs=[pl.BlockSpec(memory_space=pltpu.SMEM), vmem, vmem, vmem, vmem],
        out_specs=(vmem,) * 2,
        out_shape=(out,) * 2,
        name="pick",
        compiler_params=pltpu.CompilerParams(vmem_limit_bytes=60 * 2**20),
    )(side[None], tokens, cotangent, routed, gate)


FREE = pl.CostEstimate(flops=0, transcendentals=0, bytes_accessed=0)
STEP = 512


def rows_to_units(rows, up_mine, up_other, down_mine, down_other, units, up_sum, grad_sum):
    parts, tall, _ = rows.shape
    n = tall // 2
    step = pl.program_id(0)
    wide_up = jnp.concatenate([up_mine[...], up_other[...]], axis=1)
    wide_down = jnp.concatenate([down_mine[...], down_other[...]], axis=0)
    rows_t = jnp.concatenate([rows[k, :n] for k in range(parts)], axis=0)
    rows_g = jnp.concatenate([rows[k, n:] for k in range(parts)], axis=0)
    more_up = jnp.dot(rows_t, wide_up, preferred_element_type=FL)
    more_grad = lax.dot_general(rows_g, wide_down, (((1,), (1,)), ((), ())), preferred_element_type=FL)

    @pl.when(step == 0)
    def _():
        up_sum[...] = more_up
        grad_sum[...] = more_grad

    @pl.when(step > 0)
    def _():
        up_sum[...] += more_up
        grad_sum[...] += more_grad

    @pl.when(step == pl.num_programs(0) - 1)
    def _():
        up = up_sum[...]
        sigma = 1.0 / (1.0 + jnp.exp(-up))
        slots = up.shape[0]
        units[:slots] = (up * sigma).astype(BF)
        units[slots:] = (grad_sum[...] * sigma * (1.0 + up * (1.0 - sigma))).astype(BF)


def contracted(name, shape, rows, *weights):
    parts, tall, width = rows.shape
    hid = weights[0].shape[1]
    tall_part = pl.BlockSpec((STEP, hid), lambda k: (k, 0))
    wide_part = pl.BlockSpec((hid, STEP), lambda k: (0, k))
    total = pltpu.VMEM((shape[0] // 2, shape[1]), FL)
    return pl.pallas_call(
        rows_to_units,
        grid=(width // STEP,),
        in_specs=[pl.BlockSpec((parts, tall, STEP), lambda k: (0, 0, k)), tall_part, tall_part, wide_part, wide_part],
        out_specs=pl.BlockSpec(shape, lambda k: (0, 0)),
        out_shape=jax.ShapeDtypeStruct(shape, BF),
        scratch_shapes=[total, total],
        name=name,
        cost_estimate=FREE,
        compiler_params=pltpu.CompilerParams(vmem_limit_bytes=20 * 2**20),
    )(rows, *weights)


def shards(tokens, cotangent, routed, gate, up_weight, down_weight):
    members = lax.axis_size("expert")
    sections = lax.axis_size("pipe")
    width = tokens.shape[2]
    half = width // 2
    hid = up_weight.shape[1]

    def across(name, value, z_mask=0, x_mask=0, core_mask=0):
        flip = z_mask * 8 + x_mask * 2 + core_mask
        with jax.named_scope(name):
            return lax.ppermute(value, "expert", [(s, s ^ flip) for s in range(members)])

    def mirrored(name, value):
        with jax.named_scope(name):
            return lax.ppermute(value, "pipe", [(q, q ^ (sections // 2)) for q in range(sections)])

    def after(value, other):
        return lax.optimization_barrier((value, other))

    member = lax.axis_index("expert")
    side = (member >= members // 2).astype(jnp.int32)
    upper = (lax.axis_index("pipe") >= sections // 2).astype(jnp.int32)
    own_start = upper * half
    sent_start = (1 - upper) * half

    def columns(value, start):
        return lax.dynamic_slice_in_dim(value, start, half, 1)

    own, other = picked(side, tokens[0], cotangent[0], routed[0].T, gate[0].T)

    circles = [[z + 2 * x for x in range(4)] for z in [8 * (k // 2) + k % 2 for k in range(members // 4)]]

    def repeated(block):
        return jnp.broadcast_to(block[None], (4, *block.shape))

    def around(tag, copies):
        with jax.named_scope(tag):
            return lax.all_to_all(copies, "expert", 0, 0, axis_index_groups=circles, tiled=True)

    def ring(tag, block):
        return around(tag, repeated(block))

    other_up = across("weight_up", up_weight, core_mask=1)
    other_down = across("weight_down", down_weight, core_mask=1)
    far = across("far", other, z_mask=2)
    beside = across("beside", own, z_mask=1)
    far_beside = across("far_beside", far, z_mask=1)
    far_beside, other_up, other_down = lax.optimization_barrier((far_beside, other_up, other_down))

    def joined(first, second):
        return jnp.concatenate([first[:CAP], second[:CAP], first[CAP:], second[CAP:]], axis=0)

    near = joined(own, far)
    sent, far_beside = after(columns(near, sent_start), far_beside)
    pair = joined(beside, far_beside)
    near_ring = ring("near_ring", near)
    pair_ring = ring("pair_ring", pair)
    n = 2 * CAP
    slots = 8 * CAP

    def through(name, rows, *weights):
        return contracted(name, (2 * slots, 2 * hid), rows, *weights)

    near_units = through("near_units", near_ring, up_weight, other_up, down_weight, other_down)
    near_sent = mirrored("units_near", near_units)
    other_down, near_units = after(other_down, near_units)
    pair_units = through("pair_units", pair_ring, up_weight, other_up, down_weight, other_down)

    mirror_near = mirrored("rows_mirror", sent)
    mirror_near, near_units = after(mirror_near, near_units)
    mirror_pair = across("pair_m", mirror_near, z_mask=1)
    mirror_pair, pair_units = after(mirror_pair, pair_units)
    mirror_copies, pair_units, pair_ring = lax.optimization_barrier(
        (repeated(jnp.concatenate([mirror_near, mirror_pair], axis=0)), pair_units, pair_ring)
    )
    mirror_ring = around("mirror_ring", mirror_copies)
    pair_cols, pair_units = after(lax.dynamic_slice_in_dim(pair_ring[:, n:], own_start, half, 2), pair_units)
    pair_sent = mirrored("units_pair", pair_units)
    near_ring, near_units = after(near_ring, near_units)
    near_sent, pair_sent, mirror_ring = lax.optimization_barrier((near_sent, pair_sent, mirror_ring))

    def own_columns(part, at):
        return lax.dynamic_slice_in_dim(part[:, at : at + n], own_start, half, 2)

    def gathered(at):
        own = [own_columns(near_ring, at), own_columns(pair_ring, at) if at == 0 else pair_cols]
        sent = [mirror_ring[:, at + k : at + k + n] for k in (0, 2 * n)]
        return jnp.concatenate([part.reshape(slots, half) for part in own + sent], axis=0)

    all_t = gathered(0)
    all_g = gathered(n)
    units = (near_units, pair_units, near_sent, pair_sent)
    all_hidden = jnp.concatenate([part[:slots] for part in units], axis=0)
    all_act = jnp.concatenate([part[slots:] for part in units], axis=0)
    down = lax.dot_general(all_hidden, all_g, (((0,), (0,)), ((), ())), preferred_element_type=FL)
    down_in = across("down_swap", down[hid:].astype(BF), core_mask=1)
    raise_ = lax.dot_general(all_t, all_act, (((0,), (0,)), ((), ())), preferred_element_type=FL)
    up_in = across("up_swap", raise_[:, hid:].astype(BF), core_mask=1)
    down_out = (down[:hid] + down_in.astype(FL)).astype(BF)
    up_out = (raise_[:, :hid] + up_in.astype(FL)).astype(BF)
    return up_out[None], down_out[None]


def solution(mesh):
    in_specs = (
        P("pipe", "expert", None),
        P("pipe", "expert", None),
        P("pipe", "expert", None),
        P("pipe", "expert", None),
        P(None, "expert"),
        P("expert", None),
    )
    out_specs = (P("pipe", None, "expert"), P("pipe", "expert", None))
    return jax.shard_map(shards, mesh=mesh, in_specs=in_specs, out_specs=out_specs, check_vma=False)
```

```python
import jax
import jax.numpy as jnp
from jax import lax
from jax.experimental import pallas as pl
from jax.experimental.pallas import tpu as pltpu
from jax.sharding import PartitionSpec as P

CAP = 16
BF = jnp.bfloat16
FL = jnp.float32


def pick_rows(side_ref, tok_ref, cot_ref, routed_ref, gate_ref, own_ref, other_ref):
    side = side_ref[0]
    tokens = tok_ref.shape[0]
    routed = routed_ref[...]
    row_id = lax.broadcasted_iota(jnp.int32, (tokens, tokens), 0)
    col_id = lax.broadcasted_iota(jnp.int32, (tokens, tokens), 1)
    upper = jnp.where(row_id <= col_id, 1.0, 0.0).astype(BF)
    count = jnp.dot(routed.astype(FL).astype(BF), upper, preferred_element_type=FL)
    slot = count.astype(jnp.int32) - 1
    slot_ids = lax.broadcasted_iota(jnp.int32, (CAP, tokens), 0)

    def chosen(e):
        return (routed[e : e + 1] == 1) & (slot[e : e + 1] == slot_ids)

    first, second = chosen(0), chosen(1)
    gates = gate_ref[...]
    lean = jnp.full((CAP, tokens), side, jnp.int32) == 0
    one = jnp.where(first, 1.0, 0.0)
    two = jnp.where(second, 1.0, 0.0)
    mine = jnp.where(lean, one, two)
    rest = jnp.where(lean, two, one)
    gate_one = jnp.where(first, gates[0:1], 0.0)
    gate_two = jnp.where(second, gates[1:2], 0.0)
    gate_mine = jnp.sum(jnp.where(lean, gate_one, gate_two), axis=1, keepdims=True)
    gate_rest = jnp.sum(jnp.where(lean, gate_two, gate_one), axis=1, keepdims=True)
    picker = jnp.concatenate([mine, rest], axis=0).astype(BF)
    scale = jnp.concatenate([gate_mine, gate_rest], axis=0)
    rows = jnp.dot(picker, tok_ref[...], preferred_element_type=FL).astype(BF)
    own_ref[:CAP] = rows[:CAP]
    other_ref[:CAP] = rows[CAP:]
    grads = (jnp.dot(picker, cot_ref[...], preferred_element_type=FL) * scale).astype(BF)
    own_ref[CAP:] = grads[:CAP]
    other_ref[CAP:] = grads[CAP:]


def picked(side, tokens, cotangent, routed, gate):
    vmem = pl.BlockSpec(memory_space=pltpu.VMEM)
    out = jax.ShapeDtypeStruct((2 * CAP, tokens.shape[1]), BF)
    return pl.pallas_call(
        pick_rows,
        in_specs=[pl.BlockSpec(memory_space=pltpu.SMEM), vmem, vmem, vmem, vmem],
        out_specs=(vmem,) * 2,
        out_shape=(out,) * 2,
        name="pick",
        compiler_params=pltpu.CompilerParams(vmem_limit_bytes=60 * 2**20),
    )(side[None], tokens, cotangent, routed, gate)


FREE = pl.CostEstimate(flops=0, transcendentals=0, bytes_accessed=0)
STEP = 1792


def rows_to_units(rows, up_mine, up_other, down_mine, down_other, units):
    parts, tall, width = rows.shape
    n = tall // 2
    up = grad = None
    for at in range(0, width, STEP):
        span = slice(at, at + STEP)
        wide_up = jnp.concatenate([up_mine[span], up_other[span]], axis=1)
        wide_down = jnp.concatenate([down_mine[:, span], down_other[:, span]], axis=0)
        rows_t = jnp.concatenate([rows[k, :n, span] for k in range(parts)], axis=0)
        rows_g = jnp.concatenate([rows[k, n:, span] for k in range(parts)], axis=0)
        more_up = jnp.dot(rows_t, wide_up, preferred_element_type=FL)
        more_grad = lax.dot_general(rows_g, wide_down, (((1,), (1,)), ((), ())), preferred_element_type=FL)
        up = more_up if up is None else up + more_up
        grad = more_grad if grad is None else grad + more_grad
    sigma = 1.0 / (1.0 + jnp.exp(-up))
    slots = up.shape[0]
    units[:slots] = (up * sigma).astype(BF)
    units[slots:] = (grad * sigma * (1.0 + up * (1.0 - sigma))).astype(BF)


def in_vmem(kernel, name, shape, *operands):
    vmem = pl.BlockSpec(memory_space=pltpu.VMEM)
    return pl.pallas_call(
        kernel,
        in_specs=[vmem] * len(operands),
        out_specs=vmem,
        out_shape=jax.ShapeDtypeStruct(shape, BF),
        name=name,
        cost_estimate=FREE,
        compiler_params=pltpu.CompilerParams(vmem_limit_bytes=20 * 2**20),
    )(*operands)


def shards(tokens, cotangent, routed, gate, up_weight, down_weight):
    members = lax.axis_size("expert")
    sections = lax.axis_size("pipe")
    width = tokens.shape[2]
    half = width // 2
    hid = up_weight.shape[1]

    def across(name, value, z_mask=0, x_mask=0, core_mask=0):
        flip = z_mask * 8 + x_mask * 2 + core_mask
        with jax.named_scope(name):
            return lax.ppermute(value, "expert", [(s, s ^ flip) for s in range(members)])

    def mirrored(name, value):
        with jax.named_scope(name):
            return lax.ppermute(value, "pipe", [(q, q ^ (sections // 2)) for q in range(sections)])

    def after(value, other):
        return lax.optimization_barrier((value, other))

    member = lax.axis_index("expert")
    side = (member >= members // 2).astype(jnp.int32)
    upper = (lax.axis_index("pipe") >= sections // 2).astype(jnp.int32)
    own_start = upper * half
    sent_start = (1 - upper) * half

    def columns(value, start):
        return lax.dynamic_slice_in_dim(value, start, half, 1)

    own, other = picked(side, tokens[0], cotangent[0], routed[0].T, gate[0].T)

    circles = [[z + 2 * x for x in range(4)] for z in [8 * (k // 2) + k % 2 for k in range(members // 4)]]

    def repeated(block):
        return jnp.broadcast_to(block[None], (4, *block.shape))

    def around(tag, copies):
        with jax.named_scope(tag):
            return lax.all_to_all(copies, "expert", 0, 0, axis_index_groups=circles, tiled=True)

    def ring(tag, block):
        return around(tag, repeated(block))

    other_up = across("weight_up", up_weight, core_mask=1)
    other_down = across("weight_down", down_weight, core_mask=1)
    far = across("far", other, z_mask=2)
    beside = across("beside", own, z_mask=1)
    far_beside = across("far_beside", far, z_mask=1)
    far_beside, other_up, other_down = lax.optimization_barrier((far_beside, other_up, other_down))

    def joined(first, second):
        return jnp.concatenate([first[:CAP], second[:CAP], first[CAP:], second[CAP:]], axis=0)

    near = joined(own, far)
    sent, far_beside = after(columns(near, sent_start), far_beside)
    pair = joined(beside, far_beside)
    near_ring = ring("near_ring", near)
    pair_ring = ring("pair_ring", pair)
    n = 2 * CAP
    slots = 8 * CAP

    def through(name, rows, *weights):
        return in_vmem(rows_to_units, name, (2 * slots, 2 * hid), rows, *weights)

    near_units = through("near_units", near_ring, up_weight, other_up, down_weight, other_down)
    near_sent = mirrored("units_near", near_units)
    other_down, near_units = after(other_down, near_units)
    pair_units = through("pair_units", pair_ring, up_weight, other_up, down_weight, other_down)

    mirror_near = mirrored("rows_mirror", sent)
    mirror_near, near_units = after(mirror_near, near_units)
    mirror_pair = across("pair_m", mirror_near, z_mask=1)
    mirror_pair, pair_units = after(mirror_pair, pair_units)
    mirror_copies, pair_units, pair_ring = lax.optimization_barrier(
        (repeated(jnp.concatenate([mirror_near, mirror_pair], axis=0)), pair_units, pair_ring)
    )
    mirror_ring = around("mirror_ring", mirror_copies)
    pair_cols, pair_units = after(lax.dynamic_slice_in_dim(pair_ring[:, n:], own_start, half, 2), pair_units)
    pair_sent = mirrored("units_pair", pair_units)
    near_ring, near_units = after(near_ring, near_units)
    near_sent, pair_sent, mirror_ring = lax.optimization_barrier((near_sent, pair_sent, mirror_ring))

    def own_columns(part, at):
        return lax.dynamic_slice_in_dim(part[:, at : at + n], own_start, half, 2)

    def gathered(at):
        own = [own_columns(near_ring, at), own_columns(pair_ring, at) if at == 0 else pair_cols]
        sent = [mirror_ring[:, at + k : at + k + n] for k in (0, 2 * n)]
        return jnp.concatenate([part.reshape(slots, half) for part in own + sent], axis=0)

    all_t = gathered(0)
    all_g = gathered(n)
    units = (near_units, pair_units, near_sent, pair_sent)
    all_hidden = jnp.concatenate([part[:slots] for part in units], axis=0)
    all_act = jnp.concatenate([part[slots:] for part in units], axis=0)
    down = lax.dot_general(all_hidden, all_g, (((0,), (0,)), ((), ())), preferred_element_type=FL)
    down_in = across("down_swap", down[hid:].astype(BF), core_mask=1)
    raise_ = lax.dot_general(all_t, all_act, (((0,), (0,)), ((), ())), preferred_element_type=FL)
    up_in = across("up_swap", raise_[:, hid:].astype(BF), core_mask=1)
    down_out = (down[:hid] + down_in.astype(FL)).astype(BF)
    up_out = (raise_[:, :hid] + up_in.astype(FL)).astype(BF)
    return up_out[None], down_out[None]


def solution(mesh):
    in_specs = (
        P("pipe", "expert", None),
        P("pipe", "expert", None),
        P("pipe", "expert", None),
        P("pipe", "expert", None),
        P(None, "expert"),
        P("expert", None),
    )
    out_specs = (P("pipe", None, "expert"), P("pipe", "expert", None))
    return jax.shard_map(shards, mesh=mesh, in_specs=in_specs, out_specs=out_specs, check_vma=False)
```
